32 devices in a mesh: frame: 4 (over y, x), row: 8 (over z, core).
Axes of the slice: x: 2, y: 2, z: 4, core: 2. Of those that a mesh axis runs over, the one named last changes fastest.
Arguments:
- residual_in: bfloat16 [4, 8, 64, 768], P('frame', 'row'), may hold values from -6 to 6
- q_spatial: bfloat16 [4, 8, 64, 768], P('frame', 'row'), may hold values from -250 to 250
- k_spatial: bfloat16 [4, 8, 64, 768], P('frame', 'row'), may hold values from -250 to 250
- v_spatial: bfloat16 [4, 8, 64, 768], P('frame', 'row'), may hold values from -6 to 6
- q_temporal: bfloat16 [4, 8, 64, 768], P('frame', 'row'), may hold values from -250 to 250
- k_temporal: bfloat16 [4, 8, 64, 768], P('frame', 'row'), may hold values from -250 to 250
- conv_weight: float32 [3, 3, 768], replicated, may hold values from -2 to 2
- conv_bias: float32 [768], replicated, may hold values from -3 to 3
Outputs:
- spatial_out: bfloat16 [4, 8, 64, 768], P('frame', 'row')
- block_out: bfloat16 [4, 8, 64, 768], P('frame', 'row')
The draws below stay inside these ranges and needn't reach their ends.
All inputs are finite; a program needn't handle non-finite values.
Results may differ from the reference program's by a relative error of at most 0.0061.
Values may be sent and summed in bfloat16 or wider, within the bound.
A program may use at most 64 MiB of HBM per device.

```python
import math
import jax
import jax.numpy as jnp
from jax import lax

HEADS = 12
HEAD_DIM = 64
C = 768
WIDE = 64
HEIGHT = 8
FRAMES = 4


def base_pair(key, first_salt, second_salt):
    shape = (FRAMES, HEIGHT * WIDE, HEADS * HEAD_DIM)
    queries = jnp.clip(jax.random.normal(jax.random.fold_in(key, first_salt), shape, jnp.float32) * 1.7, -6.8, 6.8)
    keys = jnp.clip(jax.random.normal(jax.random.fold_in(key, second_salt), shape, jnp.float32) * 1.7, -6.8, 6.8)
    return (queries, keys)


def spatial_pair(key):
    queries, keys = base_pair(key, 11, 12)
    return (queries.reshape(FRAMES, HEIGHT, WIDE, HEADS * HEAD_DIM), keys.reshape(FRAMES, HEIGHT, WIDE, HEADS * HEAD_DIM))


def temporal_pair(key):
    queries, keys = base_pair(key, 21, 22)
    return (queries.reshape(FRAMES, HEIGHT, WIDE, HEADS * HEAD_DIM), keys.reshape(FRAMES, HEIGHT, WIDE, HEADS * HEAD_DIM))


def draw_q_spatial(key, part):
    return spatial_pair(key)[0].astype(jnp.bfloat16)


def draw_k_spatial(key, part):
    return spatial_pair(key)[1].astype(jnp.bfloat16)


def draw_q_temporal(key, part):
    return temporal_pair(key)[0].astype(jnp.bfloat16)


def draw_k_temporal(key, part):
    return temporal_pair(key)[1].astype(jnp.bfloat16)


def block_levels(key, dims, split, smallest, top_value):
    level = 1.0
    for axis_at, parts in split:
        steps = jax.random.uniform(jax.random.fold_in(jax.random.fold_in(key, 6), axis_at), (parts,), jnp.float32, smallest / len(split), top_value / len(split))
        level = level * jnp.repeat(jnp.exp(steps), dims[axis_at] // parts).reshape((-1,) + (1,) * (len(dims) - 1 - axis_at))
    return level


def bell_draw(key, extent, width, limit, pieces=(), kind=jnp.bfloat16):
    level = block_levels(key, extent, pieces, -0.22, 0.18) if pieces else 1.0
    values = jax.random.normal(key, extent, jnp.float32) * width * level
    return jnp.minimum(jnp.maximum(values, -limit), limit).astype(kind)


def setup_inputs(seed: int = 0) -> dict:
    seeds = jax.random.split(jax.random.key(seed), 9)
    return {
        "residual_in": bell_draw(seeds[0], (FRAMES, HEIGHT, WIDE, C), 1.0, 6.0, ((0, 4), (1, 8))),
        "q_spatial": draw_q_spatial(jax.random.fold_in(seeds[8], 71), 0),
        "k_spatial": draw_k_spatial(jax.random.fold_in(seeds[8], 71), 0),
        "v_spatial": bell_draw(seeds[3], (FRAMES, HEIGHT, WIDE, C), 1.0, 6.0, ((0, 4), (1, 8))),
        "q_temporal": draw_q_temporal(jax.random.fold_in(seeds[8], 71), 0),
        "k_temporal": draw_k_temporal(jax.random.fold_in(seeds[8], 71), 0),
        "conv_weight": bell_draw(seeds[6], (3, 3, C), 0.35, 2.0, (), jnp.float32),
        "conv_bias": bell_draw(seeds[7], (C,), 0.5, 3.0, (), jnp.float32),
    }


def spatial_frame(operands):
    query_rows, key_rows, value_rows = operands
    count = HEIGHT * WIDE
    block = math.gcd(count, 512)
    keys_f = key_rows.astype(jnp.float32).reshape(count, HEADS, HEAD_DIM)
    values_f = value_rows.astype(jnp.float32).reshape(count, HEADS, HEAD_DIM)
    queries_f = query_rows.astype(jnp.float32).reshape(count // block, block, HEADS, HEAD_DIM)

    def one_block(query_block):
        scores = jnp.einsum("thd,khd->htk", query_block, keys_f) * HEAD_DIM ** -0.5
        peak = jnp.max(scores, axis=-1, keepdims=True)
        raised = jnp.exp(scores - peak)
        totals = jnp.sum(raised, axis=-1)
        weights = lax.optimization_barrier(raised.astype(jnp.bfloat16)).astype(jnp.float32)
        blended = jnp.einsum("htk,khd->htd", weights, values_f) / totals[..., None]
        return jnp.transpose(blended, (1, 0, 2)).reshape(block, HEADS * HEAD_DIM)

    return lax.map(one_block, queries_f).reshape(count, HEADS * HEAD_DIM)


def temporal_mix(queries, keys, values):
    shape5 = (FRAMES, HEIGHT, WIDE, HEADS, HEAD_DIM)
    query_f = queries.astype(jnp.float32).reshape(shape5)
    key_f = keys.astype(jnp.float32).reshape(shape5)
    value_f = values.astype(jnp.float32).reshape(shape5)
    scores = jnp.einsum("fywhd,gywhd->ywhfg", query_f, key_f) * HEAD_DIM ** -0.5
    frame_ids = jnp.arange(FRAMES)
    allowed = frame_ids[:, None] >= frame_ids[None, :]
    scores = jnp.where(allowed, scores, -1e30)
    peak = jnp.max(scores, axis=-1, keepdims=True)
    raised = jnp.exp(scores - peak)
    totals = jnp.sum(raised, axis=-1)
    weights = lax.optimization_barrier(raised.astype(jnp.bfloat16)).astype(jnp.float32)
    blended = jnp.einsum("ywhfg,gywhd->fywhd", weights, value_f) / jnp.moveaxis(totals, 3, 0)[..., None]
    return blended.reshape(FRAMES, HEIGHT, WIDE, HEADS * HEAD_DIM)


def reference(residual_in, q_spatial, k_spatial, v_spatial, q_temporal, k_temporal, conv_weight, conv_bias):
    count = HEIGHT * WIDE
    channels = HEADS * HEAD_DIM
    attended = lax.map(spatial_frame, (q_spatial.reshape(FRAMES, count, channels),
                                       k_spatial.reshape(FRAMES, count, channels),
                                       v_spatial.reshape(FRAMES, count, channels)))
    spatial_out = attended.astype(jnp.bfloat16).reshape(FRAMES, HEIGHT, WIDE, channels)
    hidden = (residual_in.astype(jnp.float32) + spatial_out.astype(jnp.float32)).astype(jnp.bfloat16)
    temporal = temporal_mix(q_temporal, k_temporal, hidden).astype(jnp.bfloat16)
    mixed = (hidden.astype(jnp.float32) + temporal.astype(jnp.float32)).astype(jnp.bfloat16)
    padded = jnp.pad(mixed.astype(jnp.float32), ((0, 0), (1, 1), (1, 1), (0, 0)))
    conv = jnp.zeros((FRAMES, HEIGHT, WIDE, channels), jnp.float32) + conv_bias
    for first in range(3):
        for second in range(3):
            conv = conv + conv_weight[first, second] * padded[:, first:first + HEIGHT, second:second + WIDE]
    block_out = (mixed.astype(jnp.float32) + jax.nn.gelu(conv)).astype(jnp.bfloat16)
    return spatial_out, block_out
```

```python
import functools
import math

import jax
import jax.numpy as jnp
from jax import lax
from jax.experimental import pallas as pl
from jax.experimental.pallas import tpu as pltpu
from jax.sharding import PartitionSpec as P

HEAD_DIM = 64
LANES = 2 * HEAD_DIM
SCALE = HEAD_DIM ** (-0.5)
LOG2E = math.log2(math.e)


def sent_tiles(rows, half, lent, z):
    chips = rows // 2
    at_end = z in (0, chips - 1)
    helps = z in (1, chips - 2)
    tiles = 2 * half
    for i in range(half):
        bound = 1 if i < lent else 0
        if z < chips - 1 - bound:
            tiles += 4 + 2 * 2 * z
        if z > bound:
            tiles += 4 + 2 * (rows - 2 * z - 2)
        if not (at_end and bound):
            tiles += 3
        if bound:
            tiles += 2 * (at_end + helps)
    return tiles


def block_kernel(
    frames, rows, chunks, tokens, lent,
    res_hbm, q_hbm, k_hbm, v_hbm, qt_hbm, kt_hbm, cw_hbm, cb_hbm,
    so_out, bo_out,
    kv, qs, ql, rs, rp, qts, ktb, hb, hp, sob, sop, sol, tsc, wts, peak, rden, mixb, cwv, cbv,
    void, hop, sent, ld, kv_recv, ql_recv, kt_recv, so_recv, h_recv, halo_recv,
):
    me_f = lax.axis_index("frame")
    me_r = lax.axis_index("row")
    half = chunks // 2
    chips = rows // 2
    z = me_r // 2
    core = me_r % 2
    pair = me_r + 1 - 2 * core
    at_end = jnp.logical_or(z == 0, z == chips - 1)
    helps = jnp.logical_or(z == 1, z == chips - 2)
    mate = z + jnp.where(jnp.logical_or(z == 0, z == chips - 2), 1, -1)
    bits = [1 << b for b in range((frames - 1).bit_length())]

    def bound(i):
        return 1 if i < lent else 0

    def has_up(i):
        return z < chips - 1 - bound(i)

    def has_down(i):
        return z > bound(i)

    def attends(i):
        return jnp.logical_not(at_end) if i < lent else z >= 0

    def lanes(c):
        if isinstance(c, int):
            return pl.ds(c * LANES, LANES)
        return pl.ds(pl.multiple_of(c * LANES, LANES), LANES)

    def mine(i):
        return core * half + i

    def other(i):
        return (1 - core) * half + i

    def cut(ref, c):
        return ref.at[0, 0, :, lanes(c)]

    def load(src, dst, sem):
        pltpu.make_async_copy(src, dst, sem).start()

    def drain(ref, sem):
        pltpu.make_async_copy(ref, ref, sem).wait()

    def take(tiles, sem):
        drain(void.at[pl.ds(0, tiles)], sem)

    def take_per_frame(tiles, sem):
        for g in range(frames):
            if tiles(g):
                @pl.when(me_f == g)
                def _(g=g):
                    take(tiles(g), sem)

    for i in range(half):
        @pl.when(attends(i))
        def _(i=i):
            load(cut(k_hbm, mine(i)), kv.at[me_r, i, 0], kv_recv.at[me_r, i])
            load(cut(v_hbm, mine(i)), kv.at[me_r, i, 1], kv_recv.at[me_r, i])
    for i in range(half):
        load(cut(q_hbm, mine(i)), qs.at[core, i], ld.at[0])
    for c in range(chunks):
        load(cut(kt_hbm, c), ktb.at[me_f, c], ld.at[1])
    for c in range(chunks):
        load(cut(qt_hbm, c), qts.at[c], ld.at[2])
        load(cut(res_hbm, c), rs.at[c], ld.at[0])
    load(cw_hbm, cwv, ld.at[3])
    load(cb_hbm, cbv, ld.at[4])

    def signal(sem, **where):
        pl.semaphore_signal(sem, inc=1, device_id=where, device_id_type=pl.DeviceIdType.MESH)

    def hear(sem, count):
        @pl.when(count > 0)
        def _():
            pl.semaphore_wait(sem, count)

    def over(b):
        return (me_f // b) % 2 == 0

    n_over = sum(over(b).astype(jnp.int32) for b in bits)
    n_under = len(bits) - n_over

    def tell_under(sem):
        for b in bits:
            @pl.when(jnp.logical_not(over(b)))
            def _(b=b):
                signal(sem, frame=me_f - b)

    barrier = pltpu.get_barrier_semaphore()
    signal(barrier, row=pair)

    @pl.when(z < chips - 1)
    def _():
        for k in range(2):
            signal(barrier, row=2 * (z + 1) + k)

    for b in bits:
        @pl.when(over(b))
        def _(b=b):
            signal(barrier, frame=me_f + b)

    pl.semaphore_wait(barrier, 1 + 2 * (z > 0).astype(jnp.int32) + n_under)

    @pl.when(z > 0)
    def _():
        for k in range(2):
            signal(hop.at[0], row=2 * (z - 1) + k)

    tell_under(hop.at[1])

    def remote(src, dst, send, recv, **where):
        return pltpu.make_async_remote_copy(
            src_ref=src, dst_ref=dst, send_sem=send, recv_sem=recv,
            device_id=where, device_id_type=pl.DeviceIdType.MESH,
        )

    def own_kv(i, p, row):
        for which, ref in enumerate((k_hbm, v_hbm)):
            remote(
                cut(ref, p * half + i), kv.at[me_r, i, which], sent.at[0], kv_recv.at[me_r, i], row=row
            ).start()

    def lend():
        for j in range(lent):
            for p in range(2):
                remote(
                    cut(q_hbm, p * half + j), ql.at[core, j], sent.at[0], ql_recv,
                    row=2 * mate + p,
                ).start()

    def kt_copy(g, to):
        return remote(ktb.at[g], ktb.at[g], sent.at[1], kt_recv, frame=to)

    for i in range(half):
        @pl.when(has_down(i))
        def _(i=i):
            for p in range(2):
                own_kv(i, p, 2 * (z - 1) + p)

        if i == 0 and lent:
            @pl.when(z == chips - 1)
            def _():
                lend()

    for i in range(half):
        @pl.when(attends(i))
        def _(i=i):
            own_kv(i, 1 - core, pair)

        remote(cut(q_hbm, other(i)), qs.at[core, i], sent.at[0], ld.at[0], row=pair).start()
        remote(cut(res_hbm, other(i)), rp.at[i], sent.at[0], ld.at[0], row=pair).start()

    @pl.when(z < chips - 1)
    def _():
        pl.semaphore_wait(hop.at[0], 2)

    for i in range(half):
        @pl.when(has_up(i))
        def _(i=i):
            for p in range(2):
                own_kv(i, p, 2 * (z + 1) + p)

        if i == 0 and lent:
            @pl.when(z == 0)
            def _():
                lend()

    drain(ktb.at[me_f], ld.at[1])
    depth = len(bits)
    hops = 2 + depth if depth < 3 else 3 * depth

    def above(m):
        return functools.reduce(jnp.logical_and, [over(b) for b in bits if m & b])

    def below(m):
        return functools.reduce(jnp.logical_and, [jnp.logical_not(over(b)) for b in bits if m & b])

    for level in range(depth):
        hear(hop.at[1 + level], n_over)
        if level + 1 < depth:
            tell_under(hop.at[2 + level])
        for m in range(1, frames):
            if bin(m).count("1") == level + 1:
                @pl.when(above(m))
                def _(m=m):
                    kt_copy(me_f, me_f + m).start()

    if depth > 2:
        for level in range(depth - 2):
            for b in bits:
                @pl.when(over(b))
                def _(b=b, level=level):
                    signal(hop.at[1 + depth + level], frame=me_f + b)

            hear(hop.at[1 + depth + level], n_under)
        for level in range(depth):
            tell_under(hop.at[2 * depth - 1 + level])
            hear(hop.at[2 * depth - 1 + level], n_over)

    for m in range(1, frames):
        for n in range(1, m):
            if m & n == 0:
                @pl.when(jnp.logical_and(above(m), below(n)))
                def _(m=m, n=n):
                    kt_copy(me_f, me_f + m - n).start()

    signal(hop.at[hops - 1], row=pair)

    def pass_kv(src, i, side):
        return remote(
            kv.at[src, i], kv.at[src, i], sent.at[0], kv_recv.at[src, i],
            row=me_r + 2 - 4 * side,
        )

    def relay(d, i):
        @pl.when(jnp.logical_and(z + d < chips, has_down(i)))
        def _():
            for k in range(2):
                src = 2 * (z + d) + k
                pass_kv(src, i, 1).wait_recv()
                pass_kv(src, i, 1).start()

        @pl.when(jnp.logical_and(z - d >= 0, has_up(i)))
        def _():
            for k in range(2):
                src = 2 * (z - d) + k
                pass_kv(src, i, 0).wait_recv()
                pass_kv(src, i, 0).start()

    last = jnp.maximum(z, chips - 1 - z)

    @pl.loop(1, jnp.where(at_end, 1, last))
    def _(d):
        for i in range(half):
            relay(d, i)

    def score_frames():
        drain(qts, ld.at[2])

        take_per_frame(lambda g: g * chunks, kt_recv)

        flat = chunks * tokens
        same = (
            (lax.broadcasted_iota(jnp.int32, (2 * LANES, LANES), 0) // HEAD_DIM) % 2
            == lax.broadcasted_iota(jnp.int32, (2 * LANES, LANES), 1) // HEAD_DIM
        )
        spread = jnp.where(same, 1.0, 0.0).astype(jnp.bfloat16)
        peak[...] = jnp.full(peak.shape, -1e30, jnp.float32)

        @pl.loop(0, me_f + 1)
        def _(g):
            product = (
                qts[...].reshape(flat, LANES).astype(jnp.float32)
                * ktb[g].reshape(flat, LANES).astype(jnp.float32)
            )
            high = product.astype(jnp.bfloat16)
            low = (product - high.astype(jnp.float32)).astype(jnp.bfloat16)
            score = jnp.dot(
                jnp.concatenate([high, low], axis=1), spread, preferred_element_type=jnp.float32
            )
            tsc[g] = score
            peak[...] = jnp.maximum(peak[...], score)

        rden[...] = jnp.zeros(rden.shape, jnp.float32)

        @pl.loop(0, me_f + 1)
        def _(g):
            raised = jnp.exp2((tsc[g] - peak[...]) * (SCALE * LOG2E))
            rden[...] += raised
            wts[g] = raised.astype(jnp.bfloat16)

        rden[...] = 1.0 / rden[...]

    @pl.when(at_end)
    def _():
        score_frames()

    pl.semaphore_wait(hop.at[hops - 1], 1)
    take(3 * half + chunks, ld.at[0])
    first_head = lax.broadcasted_iota(jnp.int32, (tokens, LANES), 1) < HEAD_DIM
    keys = rows * tokens

    def attend(blocks, i):
        none = jnp.zeros_like(blocks[0])
        queries = jnp.concatenate(
            [part for q in blocks
             for part in (jnp.where(first_head, q, none), jnp.where(first_head, none, q))],
            axis=0,
        )
        scores = lax.dot_general(
            queries, kv[:, i, 0].reshape(keys, LANES), (((1,), (1,)), ((), ())),
            preferred_element_type=jnp.float32,
        )
        top = jnp.max(scores, axis=1, keepdims=True)
        raised = jnp.exp2((scores - top) * (SCALE * LOG2E))
        denom = jnp.sum(raised, axis=1, keepdims=True)
        both = jnp.dot(
            raised.astype(jnp.bfloat16), kv[:, i, 1].reshape(keys, LANES),
            preferred_element_type=jnp.float32,
        ) / denom
        return [
            jnp.where(
                first_head,
                both[2 * b * tokens : (2 * b + 1) * tokens],
                both[(2 * b + 1) * tokens : (2 * b + 2) * tokens],
            ).astype(jnp.bfloat16)
            for b in range(len(blocks))
        ]

    def add(a, b):
        return (a.astype(jnp.float32) + b.astype(jnp.float32)).astype(jnp.bfloat16)

    def so_copy(i, c):
        return remote(sop.at[i], sob.at[c], sent.at[0], so_recv.at[i], row=pair)

    def sol_copy(i, k, c):
        return remote(sol.at[i, k], sob.at[c], sent.at[0], so_recv.at[i], row=2 * mate + k)

    def h_copy(src, to, row, i, c):
        return remote(
            src, hb.at[me_f, c], sent.at[1], h_recv.at[i], frame=to, row=row
        )

    def arrive(i):
        @pl.when(jnp.logical_not(at_end))
        def _():
            relay(last, i)

        @pl.when(attends(i))
        def _():
            drain(kv.at[me_r, i], kv_recv.at[me_r, i])
            remote(
                kv.at[pair, i], kv.at[pair, i], sent.at[0], kv_recv.at[pair, i], row=pair
            ).wait_recv()

            @pl.when(jnp.logical_not(has_up(i)))
            def _():
                @pl.loop(0, 2 * z)
                def _(src):
                    pass_kv(src, i, 1).wait_recv()

            @pl.when(jnp.logical_not(has_down(i)))
            def _():
                @pl.loop(2 * z + 2, rows)
                def _(src):
                    pass_kv(src, i, 0).wait_recv()

    def own(i):
        c = mine(i)
        sob[c], sop[i] = attend([qs[core, i], qs[1 - core, i]], i)
        so_copy(i, c).start()
        hb[me_f, c] = add(rs[c], sob[c])
        hp[i] = add(rp[i], sop[i])

        @pl.loop(me_f + 1, frames)
        def _(to):
            h_copy(hb.at[me_f, c], to, me_r, i, c).start()
            h_copy(hp.at[i], to, pair, i, c).start()

        so_out[0, 0, :, lanes(c)] = sob[c]

    def home(c):
        hb[me_f, c] = add(rs[c], sob[c])
        so_out[0, 0, :, lanes(c)] = sob[c]

    def settle_lent(i):
        take(2, so_recv.at[i])
        for p in range(2):
            c = p * half + i
            home(c)

            @pl.loop(me_f + 1, frames)
            def _(to, c=c):
                h_copy(hb.at[me_f, c], to, me_r, i, c).start()

    def settle(i):
        @pl.when(attends(i))
        def _():
            take(1, so_recv.at[i])
            home(other(i))

    def weigh(i):
        take_per_frame(lambda g: 2 * g, h_recv.at[i])
        for p in range(2):
            c = p * half + i
            here = pl.ds(c * tokens, tokens)

            def step(g, total, c=c, here=here):
                return total + wts[g, here].astype(jnp.float32) * hb[g, c].astype(jnp.float32)

            total = lax.fori_loop(0, me_f + 1, step, jnp.zeros((tokens, LANES), jnp.float32))
            temporal = (total * rden[here]).astype(jnp.bfloat16)
            mixb[1, c] = add(hb[me_f, c], temporal)

            @pl.when(me_r > 0)
            def _(c=c):
                halo_copy(0, i, c).start()

            @pl.when(me_r < rows - 1)
            def _(c=c):
                halo_copy(1, i, c).start()

    def halo_copy(side, i, c):
        return remote(
            mixb.at[1, c], mixb.at[2 - 2 * side, c], sent.at[2], halo_recv.at[i], row=me_r - 1 + 2 * side
        )

    edges = (me_r > 0).astype(jnp.int32) + (me_r < rows - 1).astype(jnp.int32)
    position = lax.broadcasted_iota(jnp.int32, (tokens, LANES), 0)

    def convolve(i):
        for sides in (1, 2):
            @pl.when(edges == sides)
            def _(sides=sides):
                take(2 * sides, halo_recv.at[i])

        for p in range(2):
            c = p * half + i
            lines = [mixb[a, c].astype(jnp.float32) for a in range(3)]
            taps = [
                sum(cwv[a, pl.ds(b, 1), lanes(c)] * lines[a] for a in range(3)) for b in range(3)
            ]
            left = jnp.where(position == 0, 0.0, pltpu.roll(taps[0], 1, 0))
            right = jnp.where(position == tokens - 1, 0.0, pltpu.roll(taps[2], tokens - 1, 0))
            conv = cbv[pl.ds(c * LANES, LANES)].reshape(1, LANES) + taps[1] + left + right
            inner = math.sqrt(2.0 / math.pi) * (conv + 0.044715 * (conv * conv * conv))
            bo_out[0, 0, :, lanes(c)] = (
                lines[1] + 0.5 * conv * (1.0 + jnp.tanh(inner))
            ).astype(jnp.bfloat16)

    @pl.when(me_r == 0)
    def _():
        mixb[0] = jnp.zeros(mixb.shape[1:], mixb.dtype)

    @pl.when(me_r == rows - 1)
    def _():
        mixb[2] = jnp.zeros(mixb.shape[1:], mixb.dtype)

    if lent:
        @pl.when(at_end)
        def _():
            for i in range(lent):
                settle_lent(i)

    for i in range(half):
        arrive(i)
        if i < lent:
            @pl.when(helps)
            def _(i=i):
                if i == 0:
                    drain(ql, ql_recv)
                sol[i, 0], sol[i, 1] = attend([ql[0, i], ql[1, i]], i)
                for k in range(2):
                    sol_copy(i, k, mine(i)).start()

            @pl.when(jnp.logical_not(at_end))
            def _(i=i):
                own(i)
        else:
            own(i)

    @pl.when(jnp.logical_not(at_end))
    def _():
        score_frames()

    drain(cwv, ld.at[3])
    drain(cbv, ld.at[4])
    for i in range(half):
        settle(i)
        weigh(i)
    for i in range(half):
        convolve(i)
    for s in range(chips):
        @pl.when(z == s)
        def _(s=s):
            take(sent_tiles(rows, half, lent, s), sent.at[0])

    take_per_frame(lambda g: (frames - 1 - g) * 2 * chunks, sent.at[1])
    for sides in (1, 2):
        @pl.when(edges == sides)
        def _(sides=sides):
            take(sides * chunks, sent.at[2])


def store_kernel(so, bo, so_hbm, bo_hbm, sem):
    copies = [
        pltpu.make_async_copy(so, so_hbm, sem.at[0]),
        pltpu.make_async_copy(bo, bo_hbm, sem.at[1]),
    ]
    for copy in copies:
        copy.start()
    for copy in copies:
        copy.wait()


def on_device(frames, rows, *args):
    block = args[0]
    _, _, tokens, channels = block.shape
    chunks = channels // LANES
    half = chunks // 2
    chips = rows // 2
    lent = 1 if chips >= 4 else 0
    held = max(lent, 1)
    tile = (tokens, LANES)
    slab = (chunks,) + tile
    flat = (chunks * tokens, LANES)
    bf16, f32 = jnp.bfloat16, jnp.float32
    dma = pltpu.SemaphoreType.DMA
    anywhere = pl.BlockSpec(memory_space=pl.ANY)
    vmem = pl.BlockSpec(memory_space=pltpu.VMEM)
    outs = (jax.ShapeDtypeStruct(block.shape, bf16),) * 2
    room = max(
        [sent_tiles(rows, half, lent, s) for s in range(chips)] + [frames * 2 * chunks]
    )
    levels = (frames - 1).bit_length()
    mixed = pl.pallas_call(
        functools.partial(block_kernel, frames, rows, chunks, tokens, lent),
        out_shape=outs,
        in_specs=[anywhere] * 8,
        out_specs=(vmem, vmem),
        scratch_shapes=[
            pltpu.VMEM((rows, half, 2) + tile, bf16),
            pltpu.VMEM((2, half) + tile, bf16),
            pltpu.VMEM((2, held) + tile, bf16),
            pltpu.VMEM(slab, bf16),
            pltpu.VMEM((half,) + tile, bf16),
            pltpu.VMEM(slab, bf16),
            pltpu.VMEM((frames,) + slab, bf16),
            pltpu.VMEM((frames,) + slab, bf16),
            pltpu.VMEM((half,) + tile, bf16),
            pltpu.VMEM(slab, bf16),
            pltpu.VMEM((half,) + tile, bf16),
            pltpu.VMEM((held, 2) + tile, bf16),
            pltpu.VMEM((frames,) + flat, f32),
            pltpu.VMEM((frames,) + flat, bf16),
            pltpu.VMEM(flat, f32),
            pltpu.VMEM(flat, f32),
            pltpu.VMEM((3,) + slab, bf16),
            pltpu.VMEM(args[6].shape, f32),
            pltpu.VMEM(args[7].shape, f32),
            pltpu.VMEM((room,) + tile, bf16),
            pltpu.SemaphoreType.REGULAR((2 + levels if levels < 3 else 3 * levels,)),
            dma((3,)), dma((5,)), dma((rows, half)), dma, dma, dma((half,)), dma((half,)), dma((half,)),
        ],
        compiler_params=pltpu.CompilerParams(collective_id=0, has_side_effects=True,
            vmem_limit_bytes=(14 << 20) + (rows << 18) + (frames << 19)),
        name="block",
    )(*[pltpu.with_memory_space_constraint(a, pltpu.HBM) for a in args])
    return pl.pallas_call(
        store_kernel,
        out_shape=outs,
        in_specs=[vmem, vmem],
        out_specs=(anywhere, anywhere),
        scratch_shapes=[dma((2,))],
        compiler_params=pltpu.CompilerParams(vmem_limit_bytes=4 << 20),
        name="store",
    )(*mixed)


def solution(mesh):
    split = P("frame", "row", None, None)
    return jax.shard_map(
        functools.partial(on_device, mesh.shape["frame"], mesh.shape["row"]),
        mesh=mesh,
        in_specs=(split,) * 6 + (P(), P()),
        out_specs=(split, split),
        check_vma=False,
    )
```

```python
import functools
import math

import jax
import jax.numpy as jnp
from jax import lax
from jax.experimental import pallas as pl
from jax.experimental.pallas import tpu as pltpu
from jax.sharding import PartitionSpec as P

HEAD_DIM = 64
LANES = 2 * HEAD_DIM
SCALE = HEAD_DIM ** (-0.5)
LOG2E = math.log2(math.e)


def sent_tiles(rows, half, lent, z):
    chips = rows // 2
    at_end = z in (0, chips - 1)
    helps = z in (1, chips - 2)
    tiles = 2 * half
    for i in range(half):
        bound = 1 if i >= half - lent else 0
        if z < chips - 1 - bound:
            tiles += 4 + 2 * 2 * z
        if z > bound:
            tiles += 4 + 2 * (rows - 2 * z - 2)
        if not (at_end and bound):
            tiles += 3
        if bound:
            tiles += 4 * at_end + 2 * helps
    return tiles


def block_kernel(
    frames, rows, chunks, tokens, lent,
    res_hbm, q_hbm, k_hbm, v_hbm, qt_hbm, kt_hbm, cw_hbm, cb_hbm,
    so_out, bo_out,
    kv, qs, ql, rl, rs, rp, qts, ktb, hb, hp, sob, sop, sol, hl, tsc, wts, peak, rden, mixb, cwv, cbv,
    void, hop, sent, ld, kv_recv, ql_recv, kt_recv, so_recv, h_recv, halo_recv,
):
    me_f = lax.axis_index("frame")
    me_r = lax.axis_index("row")
    half = chunks // 2
    chips = rows // 2
    z = me_r // 2
    core = me_r % 2
    pair = me_r + 1 - 2 * core
    at_end = jnp.logical_or(z == 0, z == chips - 1)
    helps = jnp.logical_or(z == 1, z == chips - 2)
    mate = z + jnp.where(jnp.logical_or(z == 0, z == chips - 2), 1, -1)
    bits = [1 << b for b in range((frames - 1).bit_length())]

    def bound(i):
        return 1 if i >= half - lent else 0

    def has_up(i):
        return z < chips - 1 - bound(i)

    def has_down(i):
        return z > bound(i)

    def attends(i):
        return jnp.logical_not(at_end) if bound(i) else z >= 0

    def lanes(c):
        if isinstance(c, int):
            return pl.ds(c * LANES, LANES)
        return pl.ds(pl.multiple_of(c * LANES, LANES), LANES)

    def mine(i):
        return core * half + i

    def other(i):
        return (1 - core) * half + i

    def cut(ref, c):
        return ref.at[0, 0, :, lanes(c)]

    def load(src, dst, sem):
        pltpu.make_async_copy(src, dst, sem).start()

    def drain(ref, sem):
        pltpu.make_async_copy(ref, ref, sem).wait()

    def take(tiles, sem):
        drain(void.at[pl.ds(0, tiles)], sem)

    def take_per_frame(tiles, sem):
        for g in range(frames):
            if tiles(g):
                @pl.when(me_f == g)
                def _(g=g):
                    take(tiles(g), sem)

    def signal(sem, **where):
        pl.semaphore_signal(sem, inc=1, device_id=where, device_id_type=pl.DeviceIdType.MESH)

    def hear(sem, count):
        @pl.when(count > 0)
        def _():
            pl.semaphore_wait(sem, count)

    def over(b):
        return (me_f // b) % 2 == 0

    n_over = sum(over(b).astype(jnp.int32) for b in bits)
    n_under = len(bits) - n_over

    def tell_under(sem):
        for b in bits:
            @pl.when(jnp.logical_not(over(b)))
            def _(b=b):
                signal(sem, frame=me_f - b)

    barrier = pltpu.get_barrier_semaphore()
    signal(barrier, row=pair)

    @pl.when(z < chips - 1)
    def _():
        for k in range(2):
            signal(barrier, row=2 * (z + 1) + k)

    for b in bits:
        @pl.when(over(b))
        def _(b=b):
            signal(barrier, frame=me_f + b)

    pl.semaphore_wait(barrier, 1 + 2 * (z > 0).astype(jnp.int32) + n_under)

    @pl.when(z > 0)
    def _():
        for k in range(2):
            signal(hop.at[0], row=2 * (z - 1) + k)

    tell_under(hop.at[1])

    def remote(src, dst, send, recv, **where):
        return pltpu.make_async_remote_copy(
            src_ref=src, dst_ref=dst, send_sem=send, recv_sem=recv,
            device_id=where, device_id_type=pl.DeviceIdType.MESH,
        )

    def own_kv(i, p, row):
        for which, ref in enumerate((k_hbm, v_hbm)):
            remote(
                cut(ref, p * half + i), kv.at[me_r, i, which], sent.at[0], kv_recv.at[me_r, i], row=row
            ).start()

    def lend():
        for j in range(lent):
            for p in range(2):
                c = p * half + half - lent + j
                for src, dst in ((q_hbm, ql), (res_hbm, rl)):
                    remote(
                        cut(src, c), dst.at[core, j], sent.at[0], ql_recv, row=2 * mate + p
                    ).start()

    def kt_copy(g, to):
        return remote(ktb.at[g], ktb.at[g], sent.at[1], kt_recv, frame=to)

    for i in range(half):
        @pl.when(has_down(i))
        def _(i=i):
            for p in range(2):
                own_kv(i, p, 2 * (z - 1) + p)

    for i in range(half):
        @pl.when(attends(i))
        def _(i=i):
            own_kv(i, 1 - core, pair)

        remote(cut(q_hbm, other(i)), qs.at[core, i], sent.at[0], ld.at[0], row=pair).start()
        remote(cut(res_hbm, other(i)), rp.at[i], sent.at[0], ld.at[0], row=pair).start()

    for c in range(chunks):
        load(cut(kt_hbm, c), ktb.at[me_f, c], ld.at[1])

    for i in range(half):
        @pl.when(attends(i))
        def _(i=i):
            load(cut(k_hbm, mine(i)), kv.at[me_r, i, 0], kv_recv.at[me_r, i])
            load(cut(v_hbm, mine(i)), kv.at[me_r, i, 1], kv_recv.at[me_r, i])
    for i in range(half):
        load(cut(q_hbm, mine(i)), qs.at[core, i], ld.at[0])
    for c in range(chunks):
        load(cut(qt_hbm, c), qts.at[c], ld.at[2])
        load(cut(res_hbm, c), rs.at[c], ld.at[0])
    load(cw_hbm, cwv, ld.at[3])
    load(cb_hbm, cbv, ld.at[4])

    @pl.when(z < chips - 1)
    def _():
        pl.semaphore_wait(hop.at[0], 2)

    for i in range(half):
        @pl.when(has_up(i))
        def _(i=i):
            for p in range(2):
                own_kv(i, p, 2 * (z + 1) + p)

    if lent:
        @pl.when(at_end)
        def _():
            lend()

    drain(ktb.at[me_f], ld.at[1])
    depth = len(bits)
    hops = 2 + depth if depth < 3 else 3 * depth

    def above(m):
        return functools.reduce(jnp.logical_and, [over(b) for b in bits if m & b])

    def below(m):
        return functools.reduce(jnp.logical_and, [jnp.logical_not(over(b)) for b in bits if m & b])

    for level in range(depth):
        hear(hop.at[1 + level], n_over)
        if level + 1 < depth:
            tell_under(hop.at[2 + level])
        for m in range(1, frames):
            if bin(m).count("1") == level + 1:
                @pl.when(above(m))
                def _(m=m):
                    kt_copy(me_f, me_f + m).start()

    if depth > 2:
        for level in range(depth - 2):
            for b in bits:
                @pl.when(over(b))
                def _(b=b, level=level):
                    signal(hop.at[1 + depth + level], frame=me_f + b)

            hear(hop.at[1 + depth + level], n_under)
        for level in range(depth):
            tell_under(hop.at[2 * depth - 1 + level])
            hear(hop.at[2 * depth - 1 + level], n_over)

    for m in range(1, frames):
        for n in range(1, m):
            if m & n == 0:
                @pl.when(jnp.logical_and(above(m), below(n)))
                def _(m=m, n=n):
                    kt_copy(me_f, me_f + m - n).start()

    signal(hop.at[hops - 1], row=pair)
    if lent:
        @pl.when(at_end)
        def _():
            for p in range(2):
                signal(hop.at[hops - 1], row=2 * mate + p)

    def pass_kv(src, i, side):
        return remote(
            kv.at[src, i], kv.at[src, i], sent.at[0], kv_recv.at[src, i],
            row=me_r + 2 - 4 * side,
        )

    def relay(d, i):
        @pl.when(jnp.logical_and(z + d < chips, has_down(i)))
        def _():
            for k in range(2):
                src = 2 * (z + d) + k
                pass_kv(src, i, 1).wait_recv()
                pass_kv(src, i, 1).start()

        @pl.when(jnp.logical_and(z - d >= 0, has_up(i)))
        def _():
            for k in range(2):
                src = 2 * (z - d) + k
                pass_kv(src, i, 0).wait_recv()
                pass_kv(src, i, 0).start()

    last = jnp.maximum(z, chips - 1 - z)

    @pl.loop(1, jnp.where(at_end, 1, last))
    def _(d):
        for i in range(half):
            relay(d, i)

    def score_frames():
        drain(qts, ld.at[2])

        take_per_frame(lambda g: g * chunks, kt_recv)

        flat = chunks * tokens
        same = (
            (lax.broadcasted_iota(jnp.int32, (2 * LANES, LANES), 0) // HEAD_DIM) % 2
            == lax.broadcasted_iota(jnp.int32, (2 * LANES, LANES), 1) // HEAD_DIM
        )
        spread = jnp.where(same, 1.0, 0.0).astype(jnp.bfloat16)
        peak[...] = jnp.full(peak.shape, -1e30, jnp.float32)

        @pl.loop(0, me_f + 1)
        def _(g):
            product = (
                qts[...].reshape(flat, LANES).astype(jnp.float32)
                * ktb[g].reshape(flat, LANES).astype(jnp.float32)
            )
            high = product.astype(jnp.bfloat16)
            low = (product - high.astype(jnp.float32)).astype(jnp.bfloat16)
            score = jnp.dot(
                jnp.concatenate([high, low], axis=1), spread, preferred_element_type=jnp.float32
            )
            tsc[g] = score
            peak[...] = jnp.maximum(peak[...], score)

        rden[...] = jnp.zeros(rden.shape, jnp.float32)

        @pl.loop(0, me_f + 1)
        def _(g):
            raised = jnp.exp2((tsc[g] - peak[...]) * (SCALE * LOG2E))
            rden[...] += raised
            wts[g] = raised.astype(jnp.bfloat16)

        rden[...] = 1.0 / rden[...]

    @pl.when(at_end)
    def _():
        score_frames()

    pl.semaphore_wait(hop.at[hops - 1], 1 + 2 * helps.astype(jnp.int32) if lent else 1)
    take(3 * half + chunks, ld.at[0])
    first_head = lax.broadcasted_iota(jnp.int32, (tokens, LANES), 1) < HEAD_DIM
    keys = rows * tokens

    def attend(blocks, i):
        none = jnp.zeros_like(blocks[0])
        queries = jnp.concatenate(
            [part for q in blocks
             for part in (jnp.where(first_head, q, none), jnp.where(first_head, none, q))],
            axis=0,
        )
        scores = lax.dot_general(
            queries, kv[:, i, 0].reshape(keys, LANES), (((1,), (1,)), ((), ())),
            preferred_element_type=jnp.float32,
        )
        top = jnp.max(scores, axis=1, keepdims=True)
        raised = jnp.exp2((scores - top) * (SCALE * LOG2E))
        denom = jnp.sum(raised, axis=1, keepdims=True)
        both = jnp.dot(
            raised.astype(jnp.bfloat16), kv[:, i, 1].reshape(keys, LANES),
            preferred_element_type=jnp.float32,
        ) / denom
        return [
            jnp.where(
                first_head,
                both[2 * b * tokens : (2 * b + 1) * tokens],
                both[(2 * b + 1) * tokens : (2 * b + 2) * tokens],
            ).astype(jnp.bfloat16)
            for b in range(len(blocks))
        ]

    def add(a, b):
        return (a.astype(jnp.float32) + b.astype(jnp.float32)).astype(jnp.bfloat16)

    def each_later(send):
        if frames > 4:
            @pl.loop(me_f + 1, frames)
            def _(to):
                send(to)
            return
        ways = [(m, n) for m in range(1, frames) for n in range(m) if m & n == 0]
        for m, n in sorted(ways, key=lambda way: -bin(way[0] | way[1]).count("1")):
            @pl.when(jnp.logical_and(above(m), below(n)) if n else above(m))
            def _(m=m, n=n):
                send(me_f + m - n)

    def so_copy(i, c):
        return remote(sop.at[i], sob.at[c], sent.at[0], so_recv.at[i], row=pair)

    def sol_copy(i, k, c):
        return remote(
            sol.at[i - half + lent, k], sob.at[c], sent.at[0], so_recv.at[i], row=2 * mate + k
        )

    def h_copy(src, to, row, i, c):
        return remote(
            src, hb.at[me_f, c], sent.at[1], h_recv.at[i], frame=to, row=row
        )

    def arrive(i):
        @pl.when(jnp.logical_not(at_end))
        def _():
            relay(last, i)

        @pl.when(attends(i))
        def _():
            drain(kv.at[me_r, i], kv_recv.at[me_r, i])
            remote(
                kv.at[pair, i], kv.at[pair, i], sent.at[0], kv_recv.at[pair, i], row=pair
            ).wait_recv()

            @pl.when(jnp.logical_not(has_up(i)))
            def _():
                @pl.loop(0, 2 * z)
                def _(src):
                    pass_kv(src, i, 1).wait_recv()

            @pl.when(jnp.logical_not(has_down(i)))
            def _():
                @pl.loop(2 * z + 2, rows)
                def _(src):
                    pass_kv(src, i, 0).wait_recv()

    def own(i):
        c = mine(i)
        sob[c], sop[i] = attend([qs[core, i], qs[1 - core, i]], i)
        hb[me_f, c] = add(rs[c], sob[c])
        hp[i] = add(rp[i], sop[i])

        def send(to):
            h_copy(hb.at[me_f, c], to, me_r, i, c).start()
            h_copy(hp.at[i], to, pair, i, c).start()

        each_later(send)
        so_copy(i, c).start()
        so_out[0, 0, :, lanes(c)] = sob[c]

    def home(c):
        hb[me_f, c] = add(rs[c], sob[c])
        so_out[0, 0, :, lanes(c)] = sob[c]

    def settle(i):
        if bound(i):
            @pl.when(at_end)
            def _():
                take(2, so_recv.at[i])
                for p in range(2):
                    home(p * half + i)

        @pl.when(attends(i))
        def _():
            take(1, so_recv.at[i])
            home(other(i))

    def weigh(i):
        take_per_frame(lambda g: 2 * g, h_recv.at[i])
        for p in range(2):
            c = p * half + i
            here = pl.ds(c * tokens, tokens)

            def step(g, total, c=c, here=here):
                return total + wts[g, here].astype(jnp.float32) * hb[g, c].astype(jnp.float32)

            total = lax.fori_loop(0, me_f + 1, step, jnp.zeros((tokens, LANES), jnp.float32))
            temporal = (total * rden[here]).astype(jnp.bfloat16)
            mixb[1, c] = add(hb[me_f, c], temporal)

            @pl.when(me_r > 0)
            def _(c=c):
                halo_copy(0, i, c).start()

            @pl.when(me_r < rows - 1)
            def _(c=c):
                halo_copy(1, i, c).start()

    def halo_copy(side, i, c):
        return remote(
            mixb.at[1, c], mixb.at[2 - 2 * side, c], sent.at[2], halo_recv.at[i], row=me_r - 1 + 2 * side
        )

    edges = (me_r > 0).astype(jnp.int32) + (me_r < rows - 1).astype(jnp.int32)
    position = lax.broadcasted_iota(jnp.int32, (tokens, LANES), 0)

    def convolve(i):
        for sides in (1, 2):
            @pl.when(edges == sides)
            def _(sides=sides):
                take(2 * sides, halo_recv.at[i])

        for p in range(2):
            c = p * half + i
            lines = [mixb[a, c].astype(jnp.float32) for a in range(3)]
            taps = [
                sum(cwv[a, pl.ds(b, 1), lanes(c)] * lines[a] for a in range(3)) for b in range(3)
            ]
            left = jnp.where(position == 0, 0.0, pltpu.roll(taps[0], 1, 0))
            right = jnp.where(position == tokens - 1, 0.0, pltpu.roll(taps[2], tokens - 1, 0))
            conv = cbv[pl.ds(c * LANES, LANES)].reshape(1, LANES) + taps[1] + left + right
            inner = math.sqrt(2.0 / math.pi) * (conv + 0.044715 * (conv * conv * conv))
            bo_out[0, 0, :, lanes(c)] = (
                lines[1] + 0.5 * conv * (1.0 + jnp.tanh(inner))
            ).astype(jnp.bfloat16)

    @pl.when(me_r == 0)
    def _():
        mixb[0] = jnp.zeros(mixb.shape[1:], mixb.dtype)

    @pl.when(me_r == rows - 1)
    def _():
        mixb[2] = jnp.zeros(mixb.shape[1:], mixb.dtype)

    for i in range(half):
        arrive(i)
        if bound(i):
            @pl.when(helps)
            def _(i=i):
                j = i - half + lent
                c = mine(i)
                if j == 0:
                    take(4 * lent, ql_recv)
                sol[j, 0], sol[j, 1] = attend([ql[0, j], ql[1, j]], i)
                for k in range(2):
                    hl[j, k] = add(rl[k, j], sol[j, k])

                def send(to):
                    for k in range(2):
                        h_copy(hl.at[j, k], to, 2 * mate + k, i, c).start()

                each_later(send)
                for k in range(2):
                    sol_copy(i, k, c).start()

            @pl.when(jnp.logical_not(at_end))
            def _(i=i):
                own(i)
        else:
            own(i)

    @pl.when(jnp.logical_not(at_end))
    def _():
        score_frames()

    drain(cwv, ld.at[3])
    drain(cbv, ld.at[4])
    for i in range(half):
        settle(i)
        weigh(i)
    for i in range(half):
        convolve(i)
    for s in range(chips):
        @pl.when(z == s)
        def _(s=s):
            take(sent_tiles(rows, half, lent, s), sent.at[0])

    def take_later(attended):
        take_per_frame(lambda g: (frames - 1 - g) * (chunks + 2 * attended), sent.at[1])

    if lent:
        @pl.when(at_end)
        def _():
            take_later(half - lent)

        @pl.when(helps)
        def _():
            take_later(half + lent)

        if chips > 4:
            @pl.when(jnp.logical_not(jnp.logical_or(at_end, helps)))
            def _():
                take_later(half)
    else:
        take_later(half)

    for sides in (1, 2):
        @pl.when(edges == sides)
        def _(sides=sides):
            take(sides * chunks, sent.at[2])


def store_kernel(so, bo, so_hbm, bo_hbm, sem):
    copies = [
        pltpu.make_async_copy(so, so_hbm, sem.at[0]),
        pltpu.make_async_copy(bo, bo_hbm, sem.at[1]),
    ]
    for copy in copies:
        copy.start()
    for copy in copies:
        copy.wait()


def on_device(frames, rows, *args):
    block = args[0]
    _, _, tokens, channels = block.shape
    chunks = channels // LANES
    half = chunks // 2
    chips = rows // 2
    lent = 1 if chips >= 4 else 0
    held = max(lent, 1)
    tile = (tokens, LANES)
    slab = (chunks,) + tile
    flat = (chunks * tokens, LANES)
    bf16, f32 = jnp.bfloat16, jnp.float32
    dma = pltpu.SemaphoreType.DMA
    anywhere = pl.BlockSpec(memory_space=pl.ANY)
    vmem = pl.BlockSpec(memory_space=pltpu.VMEM)
    outs = (jax.ShapeDtypeStruct(block.shape, bf16),) * 2
    room = max(
        [sent_tiles(rows, half, lent, s) for s in range(chips)] + [frames * (2 * chunks + 2 * lent)]
    )
    levels = (frames - 1).bit_length()
    mixed = pl.pallas_call(
        functools.partial(block_kernel, frames, rows, chunks, tokens, lent),
        out_shape=outs,
        in_specs=[anywhere] * 8,
        out_specs=(vmem, vmem),
        scratch_shapes=[
            pltpu.VMEM((rows, half, 2) + tile, bf16),
            pltpu.VMEM((2, half) + tile, bf16),
            pltpu.VMEM((2, held) + tile, bf16),
            pltpu.VMEM((2, held) + tile, bf16),
            pltpu.VMEM(slab, bf16),
            pltpu.VMEM((half,) + tile, bf16),
            pltpu.VMEM(slab, bf16),
            pltpu.VMEM((frames,) + slab, bf16),
            pltpu.VMEM((frames,) + slab, bf16),
            pltpu.VMEM((half,) + tile, bf16),
            pltpu.VMEM(slab, bf16),
            pltpu.VMEM((half,) + tile, bf16),
            pltpu.VMEM((held, 2) + tile, bf16),
            pltpu.VMEM((held, 2) + tile, bf16),
            pltpu.VMEM((frames,) + flat, f32),
            pltpu.VMEM((frames,) + flat, bf16),
            pltpu.VMEM(flat, f32),
            pltpu.VMEM(flat, f32),
            pltpu.VMEM((3,) + slab, bf16),
            pltpu.VMEM(args[6].shape, f32),
            pltpu.VMEM(args[7].shape, f32),
            pltpu.VMEM((room,) + tile, bf16),
            pltpu.SemaphoreType.REGULAR((2 + levels if levels < 3 else 3 * levels,)),
            dma((3,)), dma((5,)), dma((rows, half)), dma, dma, dma((half,)), dma((half,)), dma((half,)),
        ],
        compiler_params=pltpu.CompilerParams(collective_id=0, has_side_effects=True,
            vmem_limit_bytes=(14 << 20) + (rows << 18) + (frames << 19)),
        name="block",
    )(*[pltpu.with_memory_space_constraint(a, pltpu.HBM) for a in args])
    return pl.pallas_call(
        store_kernel,
        out_shape=outs,
        in_specs=[vmem, vmem],
        out_specs=(anywhere, anywhere),
        scratch_shapes=[dma((2,))],
        compiler_params=pltpu.CompilerParams(vmem_limit_bytes=4 << 20),
        name="store",
    )(*mixed)


def solution(mesh):
    split = P("frame", "row", None, None)
    return jax.shard_map(
        functools.partial(on_device, mesh.shape["frame"], mesh.shape["row"]),
        mesh=mesh,
        in_specs=(split,) * 6 + (P(), P()),
        out_specs=(split, split),
        check_vma=False,
    )
```

```python
import functools
import math

import jax
import jax.numpy as jnp
from jax import lax
from jax.experimental import pallas as pl
from jax.experimental.pallas import tpu as pltpu
from jax.sharding import PartitionSpec as P

HEAD_DIM = 64
LANES = 2 * HEAD_DIM
SCALE = HEAD_DIM ** (-0.5)
LOG2E = math.log2(math.e)


def sent_tiles(rows, half, lent, z):
    chips = rows // 2
    at_end = z in (0, chips - 1)
    helps = z in (1, chips - 2)
    tiles = 2 * half
    for i in range(half):
        bound = 1 if i >= half - lent else 0
        if z < chips - 1 - bound:
            tiles += 4 + 2 * 2 * z
        if z > bound:
            tiles += 4 + 2 * (rows - 2 * z - 2)
        if not (at_end and bound):
            tiles += 3
        if bound:
            tiles += 4 * at_end + 2 * helps
    return tiles


def block_kernel(
    frames, rows, chunks, tokens, lent,
    res_hbm, q_hbm, k_hbm, v_hbm, qt_hbm, kt_hbm, cw_hbm, cb_hbm,
    so_out, bo_out,
    kv, qs, ql, rl, rs, rp, qts, ktb, hb, hp, sob, sop, sol, hl, tsc, wts, peak, rden, mixb, cwv, cbv,
    void, hop, sent, ld, kv_recv, ql_recv, kt_recv, so_recv, h_recv, halo_recv,
):
    me_f = lax.axis_index("frame")
    me_r = lax.axis_index("row")
    half = chunks // 2
    chips = rows // 2
    z = me_r // 2
    core = me_r % 2
    pair = me_r + 1 - 2 * core
    at_end = jnp.logical_or(z == 0, z == chips - 1)
    helps = jnp.logical_or(z == 1, z == chips - 2)
    mate = z + jnp.where(jnp.logical_or(z == 0, z == chips - 2), 1, -1)
    bits = [1 << b for b in range((frames - 1).bit_length())]

    def bound(i):
        return 1 if i >= half - lent else 0

    def has_up(i):
        return z < chips - 1 - bound(i)

    def has_down(i):
        return z > bound(i)

    def attends(i):
        return jnp.logical_not(at_end) if bound(i) else z >= 0

    def lanes(c):
        if isinstance(c, int):
            return pl.ds(c * LANES, LANES)
        return pl.ds(pl.multiple_of(c * LANES, LANES), LANES)

    def mine(i):
        return core * half + i

    def other(i):
        return (1 - core) * half + i

    def cut(ref, c):
        return ref.at[0, 0, :, lanes(c)]

    def load(src, dst, sem):
        pltpu.make_async_copy(src, dst, sem).start()

    def drain(ref, sem):
        pltpu.make_async_copy(ref, ref, sem).wait()

    def take(tiles, sem):
        drain(void.at[pl.ds(0, tiles)], sem)

    def take_per_frame(tiles, sem):
        for g in range(frames):
            if tiles(g):
                @pl.when(me_f == g)
                def _(g=g):
                    take(tiles(g), sem)

    def signal(sem, **where):
        pl.semaphore_signal(sem, inc=1, device_id=where, device_id_type=pl.DeviceIdType.MESH)

    def hear(sem, count):
        @pl.when(count > 0)
        def _():
            pl.semaphore_wait(sem, count)

    def over(b):
        return (me_f // b) % 2 == 0

    n_over = sum(over(b).astype(jnp.int32) for b in bits)
    n_under = len(bits) - n_over

    def tell_under(sem):
        for b in bits:
            @pl.when(jnp.logical_not(over(b)))
            def _(b=b):
                signal(sem, frame=me_f - b)

    barrier = pltpu.get_barrier_semaphore()
    signal(barrier, row=pair)

    @pl.when(z < chips - 1)
    def _():
        for k in range(2):
            signal(barrier, row=2 * (z + 1) + k)

    for b in bits:
        @pl.when(over(b))
        def _(b=b):
            signal(barrier, frame=me_f + b)

    pl.semaphore_wait(barrier, 1 + 2 * (z > 0).astype(jnp.int32) + n_under)

    @pl.when(z > 0)
    def _():
        for k in range(2):
            signal(hop.at[0], row=2 * (z - 1) + k)

    tell_under(hop.at[1])

    def remote(src, dst, send, recv, **where):
        return pltpu.make_async_remote_copy(
            src_ref=src, dst_ref=dst, send_sem=send, recv_sem=recv,
            device_id=where, device_id_type=pl.DeviceIdType.MESH,
        )

    def own_kv(i, p, row):
        for which, ref in enumerate((k_hbm, v_hbm)):
            remote(
                cut(ref, p * half + i), kv.at[me_r, i, which], sent.at[0], kv_recv.at[me_r, i], row=row
            ).start()

    def lend():
        for j in range(lent):
            for p in range(2):
                c = p * half + half - lent + j
                for src, dst in ((q_hbm, ql), (res_hbm, rl)):
                    remote(
                        cut(src, c), dst.at[core, j], sent.at[0], ql_recv, row=2 * mate + p
                    ).start()

    def kt_copy(g, to):
        return remote(ktb.at[g], ktb.at[g], sent.at[1], kt_recv, frame=to)

    for i in range(half):
        @pl.when(has_down(i))
        def _(i=i):
            for p in range(2):
                own_kv(i, p, 2 * (z - 1) + p)

    for i in range(half):
        @pl.when(attends(i))
        def _(i=i):
            own_kv(i, 1 - core, pair)

        remote(cut(q_hbm, other(i)), qs.at[core, i], sent.at[0], ld.at[0], row=pair).start()
        remote(cut(res_hbm, other(i)), rp.at[i], sent.at[0], ld.at[0], row=pair).start()

    for c in range(chunks):
        load(cut(kt_hbm, c), ktb.at[me_f, c], ld.at[1])

    for i in range(half):
        @pl.when(attends(i))
        def _(i=i):
            load(cut(k_hbm, mine(i)), kv.at[me_r, i, 0], kv_recv.at[me_r, i])
            load(cut(v_hbm, mine(i)), kv.at[me_r, i, 1], kv_recv.at[me_r, i])
    for i in range(half):
        load(cut(q_hbm, mine(i)), qs.at[core, i], ld.at[0])
    for c in range(chunks):
        load(cut(qt_hbm, c), qts.at[c], ld.at[2])
        load(cut(res_hbm, c), rs.at[c], ld.at[0])
    load(cw_hbm, cwv, ld.at[3])
    load(cb_hbm, cbv, ld.at[4])

    @pl.when(z < chips - 1)
    def _():
        pl.semaphore_wait(hop.at[0], 2)

    for i in range(half):
        @pl.when(has_up(i))
        def _(i=i):
            for p in range(2):
                own_kv(i, p, 2 * (z + 1) + p)

    if lent:
        @pl.when(at_end)
        def _():
            lend()

    drain(ktb.at[me_f], ld.at[1])
    depth = len(bits)
    hops = 2 + depth if depth < 3 else 3 * depth

    def above(m):
        return functools.reduce(jnp.logical_and, [over(b) for b in bits if m & b])

    def below(m):
        return functools.reduce(jnp.logical_and, [jnp.logical_not(over(b)) for b in bits if m & b])

    for level in range(depth):
        hear(hop.at[1 + level], n_over)
        if level + 1 < depth:
            tell_under(hop.at[2 + level])
        for m in range(1, frames):
            if bin(m).count("1") == level + 1:
                @pl.when(above(m))
                def _(m=m):
                    kt_copy(me_f, me_f + m).start()

    if depth > 2:
        for level in range(depth - 2):
            for b in bits:
                @pl.when(over(b))
                def _(b=b, level=level):
                    signal(hop.at[1 + depth + level], frame=me_f + b)

            hear(hop.at[1 + depth + level], n_under)
        for level in range(depth):
            tell_under(hop.at[2 * depth - 1 + level])
            hear(hop.at[2 * depth - 1 + level], n_over)

    for m in range(1, frames):
        for n in range(1, m):
            if m & n == 0:
                @pl.when(jnp.logical_and(above(m), below(n)))
                def _(m=m, n=n):
                    kt_copy(me_f, me_f + m - n).start()

    signal(hop.at[hops - 1], row=pair)
    if lent:
        @pl.when(at_end)
        def _():
            for p in range(2):
                signal(hop.at[hops - 1], row=2 * mate + p)

    def pass_kv(src, i, side):
        return remote(
            kv.at[src, i], kv.at[src, i], sent.at[0], kv_recv.at[src, i],
            row=me_r + 2 - 4 * side,
        )

    def relay(d, i):
        @pl.when(jnp.logical_and(z + d < chips, has_down(i)))
        def _():
            for k in range(2):
                src = 2 * (z + d) + k
                pass_kv(src, i, 1).wait_recv()
                pass_kv(src, i, 1).start()

        @pl.when(jnp.logical_and(z - d >= 0, has_up(i)))
        def _():
            for k in range(2):
                src = 2 * (z - d) + k
                pass_kv(src, i, 0).wait_recv()
                pass_kv(src, i, 0).start()

    last = jnp.maximum(z, chips - 1 - z)

    @pl.loop(1, jnp.where(at_end, 1, last))
    def _(d):
        for i in range(half):
            relay(d, i)

    def score_frames():
        drain(qts, ld.at[2])

        take_per_frame(lambda g: g * chunks, kt_recv)

        flat = chunks * tokens
        same = (
            (lax.broadcasted_iota(jnp.int32, (2 * LANES, LANES), 0) // HEAD_DIM) % 2
            == lax.broadcasted_iota(jnp.int32, (2 * LANES, LANES), 1) // HEAD_DIM
        )
        spread = jnp.where(same, 1.0, 0.0).astype(jnp.bfloat16)
        peak[...] = jnp.full(peak.shape, -1e30, jnp.float32)

        @pl.loop(0, me_f + 1)
        def _(g):
            product = (
                qts[...].reshape(flat, LANES).astype(jnp.float32)
                * ktb[g].reshape(flat, LANES).astype(jnp.float32)
            )
            high = product.astype(jnp.bfloat16)
            low = (product - high.astype(jnp.float32)).astype(jnp.bfloat16)
            score = jnp.dot(
                jnp.concatenate([high, low], axis=1), spread, preferred_element_type=jnp.float32
            )
            tsc[g] = score
            peak[...] = jnp.maximum(peak[...], score)

        rden[...] = jnp.zeros(rden.shape, jnp.float32)

        @pl.loop(0, me_f + 1)
        def _(g):
            raised = jnp.exp2((tsc[g] - peak[...]) * (SCALE * LOG2E))
            rden[...] += raised
            wts[g] = raised.astype(jnp.bfloat16)

        rden[...] = 1.0 / rden[...]

    @pl.when(at_end)
    def _():
        score_frames()

    pl.semaphore_wait(hop.at[hops - 1], 1 + 2 * helps.astype(jnp.int32) if lent else 1)
    take(3 * half + chunks, ld.at[0])
    first_head = lax.broadcasted_iota(jnp.int32, (tokens, LANES), 1) < HEAD_DIM
    keys = rows * tokens

    def attend(blocks, i):
        none = jnp.zeros_like(blocks[0])
        queries = jnp.concatenate(
            [part for q in blocks
             for part in (jnp.where(first_head, q, none), jnp.where(first_head, none, q))],
            axis=0,
        )
        scores = lax.dot_general(
            queries, kv[:, i, 0].reshape(keys, LANES), (((1,), (1,)), ((), ())),
            preferred_element_type=jnp.float32,
        )
        top = jnp.max(scores, axis=1, keepdims=True)
        raised = jnp.exp2((scores - top) * (SCALE * LOG2E))
        denom = jnp.sum(raised, axis=1, keepdims=True)
        both = jnp.dot(
            raised.astype(jnp.bfloat16), kv[:, i, 1].reshape(keys, LANES),
            preferred_element_type=jnp.float32,
        ) / denom
        return [
            jnp.where(
                first_head,
                both[2 * b * tokens : (2 * b + 1) * tokens],
                both[(2 * b + 1) * tokens : (2 * b + 2) * tokens],
            ).astype(jnp.bfloat16)
            for b in range(len(blocks))
        ]

    def add(a, b):
        return (a.astype(jnp.float32) + b.astype(jnp.float32)).astype(jnp.bfloat16)

    def each_later(send):
        if frames > 4:
            @pl.loop(me_f + 1, frames)
            def _(to):
                send(to)
            return
        ways = [(m, n) for m in range(1, frames) for n in range(m) if m & n == 0]
        for m, n in sorted(ways, key=lambda way: way[0] - way[1]):
            @pl.when(jnp.logical_and(above(m), below(n)) if n else above(m))
            def _(m=m, n=n):
                send(me_f + m - n)

    def so_copy(i, c):
        return remote(sop.at[i], sob.at[c], sent.at[0], so_recv.at[i], row=pair)

    def sol_copy(i, k, c):
        return remote(
            sol.at[i - half + lent, k], sob.at[c], sent.at[0], so_recv.at[i], row=2 * mate + k
        )

    def h_copy(src, to, row, i, c):
        return remote(
            src, hb.at[me_f, c], sent.at[1], h_recv.at[i], frame=to, row=row
        )

    def arrive(i):
        @pl.when(jnp.logical_not(at_end))
        def _():
            relay(last, i)

        @pl.when(attends(i))
        def _():
            drain(kv.at[me_r, i], kv_recv.at[me_r, i])
            remote(
                kv.at[pair, i], kv.at[pair, i], sent.at[0], kv_recv.at[pair, i], row=pair
            ).wait_recv()

            @pl.when(jnp.logical_not(has_up(i)))
            def _():
                @pl.loop(0, 2 * z)
                def _(src):
                    pass_kv(src, i, 1).wait_recv()

            @pl.when(jnp.logical_not(has_down(i)))
            def _():
                @pl.loop(2 * z + 2, rows)
                def _(src):
                    pass_kv(src, i, 0).wait_recv()

    def own(i):
        c = mine(i)
        sob[c], sop[i] = attend([qs[core, i], qs[1 - core, i]], i)
        hb[me_f, c] = add(rs[c], sob[c])
        hp[i] = add(rp[i], sop[i])

        def send(to):
            h_copy(hb.at[me_f, c], to, me_r, i, c).start()
            h_copy(hp.at[i], to, pair, i, c).start()

        each_later(send)
        so_copy(i, c).start()
        so_out[0, 0, :, lanes(c)] = sob[c]

    def home(c):
        hb[me_f, c] = add(rs[c], sob[c])
        so_out[0, 0, :, lanes(c)] = sob[c]

    def settle(i):
        if bound(i):
            @pl.when(at_end)
            def _():
                take(2, so_recv.at[i])
                for p in range(2):
                    home(p * half + i)

        @pl.when(attends(i))
        def _():
            take(1, so_recv.at[i])
            home(other(i))

    def weigh(i):
        take_per_frame(lambda g: 2 * g, h_recv.at[i])
        for p in range(2):
            c = p * half + i
            here = pl.ds(c * tokens, tokens)

            def step(g, total, c=c, here=here):
                return total + wts[g, here].astype(jnp.float32) * hb[g, c].astype(jnp.float32)

            total = lax.fori_loop(0, me_f + 1, step, jnp.zeros((tokens, LANES), jnp.float32))
            temporal = (total * rden[here]).astype(jnp.bfloat16)
            mixb[1, c] = add(hb[me_f, c], temporal)

            @pl.when(me_r > 0)
            def _(c=c):
                halo_copy(0, i, c).start()

            @pl.when(me_r < rows - 1)
            def _(c=c):
                halo_copy(1, i, c).start()

    def halo_copy(side, i, c):
        return remote(
            mixb.at[1, c], mixb.at[2 - 2 * side, c], sent.at[2], halo_recv.at[i], row=me_r - 1 + 2 * side
        )

    edges = (me_r > 0).astype(jnp.int32) + (me_r < rows - 1).astype(jnp.int32)
    position = lax.broadcasted_iota(jnp.int32, (tokens, LANES), 0)

    def convolve(i):
        for sides in (1, 2):
            @pl.when(edges == sides)
            def _(sides=sides):
                take(2 * sides, halo_recv.at[i])

        for p in range(2):
            c = p * half + i
            lines = [mixb[a, c].astype(jnp.float32) for a in range(3)]
            taps = [
                sum(cwv[a, pl.ds(b, 1), lanes(c)] * lines[a] for a in range(3)) for b in range(3)
            ]
            left = jnp.where(position == 0, 0.0, pltpu.roll(taps[0], 1, 0))
            right = jnp.where(position == tokens - 1, 0.0, pltpu.roll(taps[2], tokens - 1, 0))
            conv = cbv[pl.ds(c * LANES, LANES)].reshape(1, LANES) + taps[1] + left + right
            inner = math.sqrt(2.0 / math.pi) * (conv + 0.044715 * (conv * conv * conv))
            bo_out[0, 0, :, lanes(c)] = (
                lines[1] + 0.5 * conv * (1.0 + jnp.tanh(inner))
            ).astype(jnp.bfloat16)

    @pl.when(me_r == 0)
    def _():
        mixb[0] = jnp.zeros(mixb.shape[1:], mixb.dtype)

    @pl.when(me_r == rows - 1)
    def _():
        mixb[2] = jnp.zeros(mixb.shape[1:], mixb.dtype)

    for i in range(half):
        arrive(i)
        if bound(i):
            @pl.when(helps)
            def _(i=i):
                j = i - half + lent
                c = mine(i)
                if j == 0:
                    take(4 * lent, ql_recv)
                sol[j, 0], sol[j, 1] = attend([ql[0, j], ql[1, j]], i)
                for k in range(2):
                    hl[j, k] = add(rl[k, j], sol[j, k])

                def send(to):
                    for k in range(2):
                        h_copy(hl.at[j, k], to, 2 * mate + k, i, c).start()

                each_later(send)
                for k in range(2):
                    sol_copy(i, k, c).start()

            @pl.when(jnp.logical_not(at_end))
            def _(i=i):
                own(i)
        else:
            own(i)

    @pl.when(jnp.logical_not(at_end))
    def _():
        score_frames()

    drain(cwv, ld.at[3])
    drain(cbv, ld.at[4])
    def finish(order):
        for i in order:
            settle(i)
            weigh(i)

    forward = list(range(half))
    swapped = forward[:-2] + forward[:-3:-1] if lent else forward

    @pl.when(at_end)
    def _():
        finish(swapped)

    @pl.when(jnp.logical_not(at_end))
    def _():
        finish(forward)

    for i in swapped:
        convolve(i)
    for s in range(chips):
        @pl.when(z == s)
        def _(s=s):
            take(sent_tiles(rows, half, lent, s), sent.at[0])

    def take_later(attended):
        take_per_frame(lambda g: (frames - 1 - g) * (chunks + 2 * attended), sent.at[1])

    if lent:
        @pl.when(at_end)
        def _():
            take_later(half - lent)

        @pl.when(helps)
        def _():
            take_later(half + lent)

        if chips > 4:
            @pl.when(jnp.logical_not(jnp.logical_or(at_end, helps)))
            def _():
                take_later(half)
    else:
        take_later(half)

    for sides in (1, 2):
        @pl.when(edges == sides)
        def _(sides=sides):
            take(sides * chunks, sent.at[2])


def store_kernel(so, bo, so_hbm, bo_hbm, sem):
    copies = [
        pltpu.make_async_copy(so, so_hbm, sem.at[0]),
        pltpu.make_async_copy(bo, bo_hbm, sem.at[1]),
    ]
    for copy in copies:
        copy.start()
    for copy in copies:
        copy.wait()


def on_device(frames, rows, *args):
    block = args[0]
    _, _, tokens, channels = block.shape
    chunks = channels // LANES
    half = chunks // 2
    chips = rows // 2
    lent = 1 if chips >= 4 else 0
    held = max(lent, 1)
    tile = (tokens, LANES)
    slab = (chunks,) + tile
    flat = (chunks * tokens, LANES)
    bf16, f32 = jnp.bfloat16, jnp.float32
    dma = pltpu.SemaphoreType.DMA
    anywhere = pl.BlockSpec(memory_space=pl.ANY)
    vmem = pl.BlockSpec(memory_space=pltpu.VMEM)
    outs = (jax.ShapeDtypeStruct(block.shape, bf16),) * 2
    room = max(
        [sent_tiles(rows, half, lent, s) for s in range(chips)] + [frames * (2 * chunks + 2 * lent)]
    )
    levels = (frames - 1).bit_length()
    mixed = pl.pallas_call(
        functools.partial(block_kernel, frames, rows, chunks, tokens, lent),
        out_shape=outs,
        in_specs=[anywhere] * 8,
        out_specs=(vmem, vmem),
        scratch_shapes=[
            pltpu.VMEM((rows, half, 2) + tile, bf16),
            pltpu.VMEM((2, half) + tile, bf16),
            pltpu.VMEM((2, held) + tile, bf16),
            pltpu.VMEM((2, held) + tile, bf16),
            pltpu.VMEM(slab, bf16),
            pltpu.VMEM((half,) + tile, bf16),
            pltpu.VMEM(slab, bf16),
            pltpu.VMEM((frames,) + slab, bf16),
            pltpu.VMEM((frames,) + slab, bf16),
            pltpu.VMEM((half,) + tile, bf16),
            pltpu.VMEM(slab, bf16),
            pltpu.VMEM((half,) + tile, bf16),
            pltpu.VMEM((held, 2) + tile, bf16),
            pltpu.VMEM((held, 2) + tile, bf16),
            pltpu.VMEM((frames,) + flat, f32),
            pltpu.VMEM((frames,) + flat, bf16),
            pltpu.VMEM(flat, f32),
            pltpu.VMEM(flat, f32),
            pltpu.VMEM((3,) + slab, bf16),
            pltpu.VMEM(args[6].shape, f32),
            pltpu.VMEM(args[7].shape, f32),
            pltpu.VMEM((room,) + tile, bf16),
            pltpu.SemaphoreType.REGULAR((2 + levels if levels < 3 else 3 * levels,)),
            dma((3,)), dma((5,)), dma((rows, half)), dma, dma, dma((half,)), dma((half,)), dma((half,)),
        ],
        compiler_params=pltpu.CompilerParams(collective_id=0, has_side_effects=True,
            vmem_limit_bytes=(14 << 20) + (rows << 18) + (frames << 19)),
        name="block",
    )(*[pltpu.with_memory_space_constraint(a, pltpu.HBM) for a in args])
    return pl.pallas_call(
        store_kernel,
        out_shape=outs,
        in_specs=[vmem, vmem],
        out_specs=(anywhere, anywhere),
        scratch_shapes=[dma((2,))],
        compiler_params=pltpu.CompilerParams(vmem_limit_bytes=4 << 20),
        name="store",
    )(*mixed)


def solution(mesh):
    split = P("frame", "row", None, None)
    return jax.shard_map(
        functools.partial(on_device, mesh.shape["frame"], mesh.shape["row"]),
        mesh=mesh,
        in_specs=(split,) * 6 + (P(), P()),
        out_specs=(split, split),
        check_vma=False,
    )
```
